512 devices in a mesh: section: 8 (over y, core), expert: 64 (over z, x).
Axes of the slice: x: 4, y: 4, z: 16, core: 2. Of those that a mesh axis runs over, the one named last changes fastest.
Arguments:
- tokens: bfloat16 [8, 4096, 4096], P('section', 'expert'), may hold values from -6 to 6
- expert_ids: int32 [8, 1, 4096, 1], P('section'), may hold values from 0 to 7; in each aligned block of 64 rows (0 to 63, 64 to 127, ..., all dimensions but the last counted through in order) at most 12 rows name the same one
- gate_weights: float32 [8, 1, 4096, 1], P('section'), may hold values from 0.2 to 1
- norm_gain: bfloat16 [8, 4096], P('section'), may hold values from 0.099609375 to 1.8984375
- w_gate: bfloat16 [8, 4096, 8192], P('section', None, 'expert'), may hold values from -0.09375 to 0.09375
- w_up: bfloat16 [8, 4096, 8192], P('section', None, 'expert'), may hold values from -0.09375 to 0.09375
- w_down: bfloat16 [8, 8192, 4096], P('section', 'expert'), may hold values from -0.1875 to 0.1875
Outputs:
- finished: bfloat16 [8, 4096, 4096], P('section', 'expert')
The draws below stay inside these ranges and needn't reach their ends.
Inputs may be any that keep to these rules, and one draw needn't show every extreme that they name: `expert_ids`: each row names one expert (1 = 1). In every aligned block of 64 rows (one device's rows at one section and stop) no expert is named by more than 12 rows, and some block names some expert exactly 12 times.
All inputs are finite; a program needn't handle non-finite values.
Results may differ from the reference program's by a relative error of at most 0.0041.
Values may be sent and summed in bfloat16 or wider, within the bound.
A program may use at most 64 MiB of HBM per device.

```python
import math
import jax
import jax.numpy as jnp
import numpy as np
from jax import lax

D = 4096
FF_WIN = 1024
EXPS = 8
TOPK = 1
STOPS = 1
ROWS_DEV = 64
CAP = 12
SECTIONS = 8
TOKS = 4096
N_EXPERT = 64


def level_of(key, shape, shards, smallest, largest):
    def one(position, shards_of):
        draws = jax.random.uniform(jax.random.fold_in(jax.random.fold_in(key, 6), position), (shards_of,), jnp.float32, smallest / len(shards), largest / len(shards))
        return jnp.repeat(jnp.exp(draws), shape[position] // shards_of).reshape((-1,) + (1,) * (len(shape) - position - 1))

    factor_of = one(*shards[0])
    for cut in shards[1:]:
        factor_of = factor_of * one(*cut)
    return factor_of


def assign_block(key, own, number, rows, count, top, reach, skew):
    sequence = jax.random.permutation(key, count)
    heavy_load, common = portions_of(count, rows * top, reach, skew, True), portions_of(count, rows * top, reach, skew, False)
    places = jnp.arange(count)

    def named(tallies, offset_by):
        used = int((tallies > 0).sum())
        fixed = max(1, used // 4)
        passed = fixed + (places - fixed + offset_by * (used - fixed)) % max(1, count - fixed)
        return jnp.zeros((count,), jnp.int32).at[sequence[jnp.where(places < fixed, places, passed)]].set(jnp.asarray(tallies, jnp.int32))

    tallies = jnp.where(number % 4 == 0, named(heavy_load, number // 4), named(common, number - number // 4 - 1))
    mixed = jax.random.permutation(jax.random.fold_in(own, 3), count)
    source_of, receiver = mixed[0:count // 2 * 2:2], mixed[1:count // 2 * 2:2]
    slack = jnp.minimum(tallies[source_of] - 1, reach - tallies[receiver]) // 2
    slack = jnp.where((source_of == sequence[0]) | (receiver == sequence[0]) | (tallies[receiver] == 0), 0, jnp.maximum(slack, 0))
    passed = jax.random.randint(jax.random.fold_in(own, 4), (count // 2,), 0, 1 << 20) % (slack + 1)
    tallies = tallies.at[source_of].add(-passed).at[receiver].add(passed)
    members = jnp.searchsorted(jnp.cumsum(tallies), jnp.arange(rows * top), side="right").astype(jnp.int32)
    table = members.reshape(top, rows).T
    table = table[jax.random.permutation(jax.random.fold_in(own, 1), rows)]
    offset_by = jax.random.randint(jax.random.fold_in(own, 2), (rows, 1), 0, top)
    return jnp.take_along_axis(table, (jnp.arange(top)[None, :] + offset_by) % top, axis=1)


def portions_of(number_of, total, limit, lean, full):
    weights = [(1 << 20) // math.isqrt(rank ** lean) + 1 for rank in range(1, number_of + 1)]
    largest = limit if full else min(limit, max(-(-total // number_of), total * weights[0] // sum(weights)))
    least = 1 if total - largest >= number_of - 1 else 0
    given, spare = [largest] + [least] * (number_of - 1), total - largest - least * (number_of - 1)
    while spare > 0:
        candidates = [i for i in range(1, number_of) if given[i] < largest] or [i for i in range(1, number_of) if given[i] < limit]
        mass, left = sum([weights[i] for i in candidates]), spare
        for i in candidates:
            more = min(limit - given[i], max(1, left * weights[i] // mass), spare)
            given[i] = given[i] + more
            spare = spare - more
    return np.array(given)


def gaussian(key, dims, scale, limit, shards=(), kind=jnp.bfloat16):
    values = scale * jax.random.normal(key, dims, jnp.float32)
    if shards:
        values = values * level_of(key, dims, shards, -0.22, 0.18)
    return jnp.clip(values, -limit, limit).astype(kind)


def setup_inputs(seed: int = 0) -> dict:
    key_list = jax.random.split(jax.random.key(seed), 8)
    tokens = gaussian(key_list[0], (SECTIONS, TOKS, D), 1.0, 6.0, ((0, 8), (1, 64)))
    expert_ids_keys = jax.random.split(jax.random.fold_in(key_list[1], 1), SECTIONS * STOPS * TOKS // ROWS_DEV)
    expert_ids_turns = jax.random.permutation(jax.random.fold_in(key_list[1], 3), SECTIONS * STOPS * TOKS // ROWS_DEV)
    expert_ids = jax.vmap(lambda own, number: assign_block(jax.random.fold_in(key_list[1], 2), own, number, ROWS_DEV, EXPS, TOPK, CAP, 2))(expert_ids_keys, expert_ids_turns).reshape((SECTIONS, STOPS, TOKS, TOPK))
    gate_weights = jnp.clip(0.2 + 0.8 * jax.random.uniform(key_list[2], (SECTIONS, STOPS, TOKS, TOPK), jnp.float32) ** level_of(key_list[2], (SECTIONS, STOPS, TOKS, TOPK), ((0, 8),), -0.2, 0.2), 0.2, 1.0)
    norm_gain = jnp.clip(1.0 + 0.18 * jax.random.normal(key_list[3], (SECTIONS, D), jnp.float32), 0.099609375, 1.8984375).astype(jnp.bfloat16)
    w_gate = gaussian(key_list[4], (SECTIONS, D, EXPS * FF_WIN), D ** -0.5, 0.09375, ((0, 8), (2, 64)))
    w_up = gaussian(key_list[5], (SECTIONS, D, EXPS * FF_WIN), D ** -0.5, 0.09375, ((0, 8), (2, 64)))
    w_down = gaussian(key_list[6], (SECTIONS, EXPS * FF_WIN, D), FF_WIN ** -0.5, 0.1875, ((0, 8), (1, 64)))
    return {"tokens": tokens, "expert_ids": expert_ids, "gate_weights": gate_weights, "norm_gain": norm_gain, "w_gate": w_gate, "w_up": w_up, "w_down": w_down}


def tables(route_ids, route_weights, blocks, row_count, width, experts, slot_cap):
    hot_map = (route_ids[:, :, None] == jnp.arange(experts, dtype=jnp.int32)).astype(jnp.int32)
    hot_map = hot_map.reshape(blocks, row_count * width, experts)
    slot_rank = jnp.cumsum(hot_map, axis=1) - 1
    chosen = hot_map[..., None] * (slot_rank[..., None] == jnp.arange(slot_cap, dtype=jnp.int32)).astype(jnp.int32)
    chosen = chosen.reshape(blocks, row_count, width, experts, slot_cap)
    placed = lax.optimization_barrier(jnp.sum(chosen, axis=2))
    scaled = lax.optimization_barrier(jnp.sum(chosen.astype(jnp.float32) * route_weights.reshape(blocks, row_count, width, 1, 1).astype(jnp.float32), axis=2))
    return (placed, scaled)

def one_expert(inputs):
    slotted, gate_cols, up_cols, down_rows = inputs
    flat_rows = slotted.reshape(-1, D)
    count_rows = flat_rows.shape[0]
    gate = jnp.dot(flat_rows, gate_cols, preferred_element_type=jnp.float32)
    upward = jnp.dot(flat_rows, up_cols, preferred_element_type=jnp.float32)
    hidden = (jax.nn.silu(gate) * upward).astype(jnp.bfloat16)
    group_count = N_EXPERT // EXPS
    group_width = FF_WIN // group_count
    partial_value = jnp.einsum('nsf,sfd->nsd', hidden.reshape(count_rows, group_count, group_width).astype(jnp.float32), down_rows.reshape(group_count, group_width, D).astype(jnp.float32), precision=lax.Precision.HIGHEST)
    partial_value = lax.optimization_barrier(partial_value.astype(jnp.bfloat16)).astype(jnp.float32)
    return lax.optimization_barrier(jnp.sum(partial_value, axis=1)).reshape(N_EXPERT, CAP, D)

def stop_layer(inputs):
    current, route_ids, route_weights, gain, gate_all, up_all, down_all = inputs
    wide_state = current.astype(jnp.float32)
    meansq = lax.optimization_barrier(jnp.mean(wide_state * wide_state, axis=-1, keepdims=True))
    normed = (wide_state * lax.rsqrt(meansq + 1e-06) * gain.astype(jnp.float32)).astype(jnp.bfloat16)
    placed, scaled = tables(route_ids, route_weights, N_EXPERT, ROWS_DEV, TOPK, EXPS, CAP)
    slotted = jnp.einsum('brec,brd->ebcd', placed.astype(jnp.float32), normed.reshape(N_EXPERT, ROWS_DEV, D).astype(jnp.float32), precision=lax.Precision.HIGHEST).astype(jnp.bfloat16)
    gate_stack = gate_all.reshape(D, EXPS, FF_WIN).transpose(1, 0, 2)
    up_stack = up_all.reshape(D, EXPS, FF_WIN).transpose(1, 0, 2)
    down_stack = down_all.reshape(EXPS, FF_WIN, D)
    results = lax.map(one_expert, (slotted, gate_stack, up_stack, down_stack))
    expert_out = jnp.einsum('brec,ebcd->brd', scaled, results, precision=lax.Precision.HIGHEST)
    return (wide_state + expert_out.reshape(TOKS, D)).astype(jnp.bfloat16)

def reference(tokens, expert_ids, gate_weights, norm_gain, w_gate, w_up, w_down):
    current = tokens
    for stop_index in range(STOPS):
        current = lax.map(stop_layer, (current, expert_ids[:, stop_index], gate_weights[:, stop_index], norm_gain, w_gate, w_up, w_down))
        current = jnp.roll(current, 1, axis=0)
    return current
```

```python
import jax
import jax.numpy as jnp
from jax import lax
from jax.experimental import pallas as pl
from jax.experimental.pallas import tpu as pltpu
from jax.sharding import PartitionSpec as P

MESH = pl.DeviceIdType.MESH
EXPS = 8
CAP = 12
NX = 4
NZ = 16
ROWS = 64
D = 4096
DX = D // NX
UNIT = NX * CAP
PLANE = NX * ROWS
HID = 128
WAVES = ((7, 3), (6, 2), (5, 1), (4, 0))
SEND_ORDER = (7, 3, 6, 2, 5, 1, 4)
PLACE = {t: (w, j) for w, pair in enumerate(WAVES) for j, t in enumerate(pair)}
F32 = jnp.float32
BF16 = jnp.bfloat16


def kernel(
    tok, ids, weights, gain, wg, wu, wd, out,
    normed, rows_in, zsend, xin, wcat, wdn, rs_send, rs_recv, hid,
    own_part, pr_send, pr_recv, ret_send, ret_recv, eo_send, eo_recv, hprev, select, column,
    loc_sem, nx_s, nx_r, wx_s, wx_r, h_s, h_r, z_s, z_r, f_s, f_r, rs_s, rs_r, hd_s, hd_r,
    pr_s, pr_r, rt_s, rt_r, eo_s, eo_r,
):
    sections = lax.axis_size("section")
    sec = lax.axis_index("section")
    me = lax.axis_index("expert")
    z = me // NX
    x = me % NX
    sign = 1 - 2 * (z % 2)
    sec_next = (sec + 1) % sections
    sec_last = (sec + sections - 1) % sections

    def at_z(offset):
        return (sec, ((z + offset + NZ) % NZ) * NX + x)

    def at_x(k):
        return (sec, z * NX + (x + k) % NX)

    def dest_offset(t):
        return 2 * sign * t if t < 4 else -sign * (2 * t - 7)

    def source_offset(t):
        return -2 * sign * t if t < 4 else -sign * (2 * t - 7)

    partner = at_z(sign)

    def remote(src, dst, ssem, rsem, device):
        return pltpu.make_async_remote_copy(
            src_ref=src, dst_ref=dst, send_sem=ssem, recv_sem=rsem,
            device_id=device, device_id_type=MESH,
        )

    pending = []

    def send(*args):
        copy = remote(*args)
        copy.start()
        pending.append(copy)

    barrier = pltpu.get_barrier_semaphore()
    others = [at_x(k) for k in (1, 2, 3)]
    others += [at_z(dest_offset(t)) for t in range(1, 8)]
    others += [at_z(source_offset(t)) for t in range(1, 4)]
    others += [partner]
    others += [(sec_next, z * NX + k) for k in range(NX)]
    others += [(sec_last, z * NX + k) for k in range(NX)]
    for other in others:
        pl.semaphore_signal(barrier, inc=1, device_id=other, device_id_type=MESH)

    own_rows = pl.ds(pl.multiple_of(x * DX, DX), DX)
    own_gate = pl.ds(pl.multiple_of(x * 2 * HID, HID), HID)
    own_up = pl.ds(pl.multiple_of(x * 2 * HID + HID, HID), HID)
    own_hid = pl.ds(pl.multiple_of(x * HID, HID), HID)
    local = [
        pltpu.make_async_copy(wg.at[own_rows, :], wcat.at[:, own_gate], loc_sem.at[0]),
        pltpu.make_async_copy(wu.at[own_rows, :], wcat.at[:, own_up], loc_sem.at[1]),
        pltpu.make_async_copy(wd.at[:, own_rows], wdn.at[own_hid, :], loc_sem.at[2]),
    ]
    for copy in local:
        copy.start()

    total = jnp.zeros((ROWS, 1), F32)
    for c in range(NX):
        part = tok[:, c * DX:(c + 1) * DX].astype(F32)
        total = total + jnp.sum(part * part, axis=1, keepdims=True)
    scale = lax.rsqrt(total / D + 1e-6)
    for c in range(NX):
        part = tok[:, c * DX:(c + 1) * DX].astype(F32)
        part = part * scale * gain[:, c * DX:(c + 1) * DX].astype(F32)
        normed[:, c * DX:(c + 1) * DX] = part.astype(BF16)

    def plane_row(ref):
        return jnp.concatenate([ref[pl.ds(2 * z, 1), :], ref[pl.ds(2 * z + 1, 1), :]], axis=1)

    ids_row = plane_row(ids)
    named = lax.broadcasted_iota(jnp.int32, (16, PLANE), 0) == ids_row
    named = jnp.where(named, 1.0, 0.0)
    early = lax.broadcasted_iota(jnp.int32, (PLANE, PLANE), 0)
    late = lax.broadcasted_iota(jnp.int32, (PLANE, PLANE), 1)
    before = jnp.where((early < late) & (early // ROWS == late // ROWS), 1.0, 0.0).astype(BF16)
    count = jnp.dot(named.astype(BF16), before, preferred_element_type=F32)
    slot = jnp.sum(named * count, axis=0, keepdims=True)
    block = lax.broadcasted_iota(jnp.int32, (1, PLANE), 1) // ROWS
    place = (ids_row * UNIT + block * CAP).astype(F32) + slot
    experts = [((z + dest_offset(t) + NZ) % NZ) // 2 for t in range(EXPS)]

    pl.semaphore_wait(barrier, len(others))

    rows_in[pl.ds(pl.multiple_of(x * ROWS, ROWS), ROWS), :] = normed[:, own_rows]
    own_block = pl.ds(pl.multiple_of(x * ROWS, ROWS), ROWS)
    for k in (1, 3, 2):
        other_cols = pl.ds(pl.multiple_of(((x + k) % NX) * DX, DX), DX)
        send(normed.at[:, other_cols], rows_in.at[own_block, :], nx_s.at[k - 1], nx_r.at[k - 1], at_x(k))
    for k in (1, 3, 2):
        other_rows = pl.ds(pl.multiple_of(((x + k) % NX) * DX, DX), DX)
        send(wg.at[other_rows, :], wcat.at[:, own_gate], wx_s.at[0, k - 1], wx_r.at[0, k - 1], at_x(k))
        send(wu.at[other_rows, :], wcat.at[:, own_up], wx_s.at[1, k - 1], wx_r.at[1, k - 1], at_x(k))
    send(tok, hprev, h_s, h_r, (sec_next, me))

    spread = []
    for t in range(EXPS):
        index = lax.broadcasted_iota(jnp.int32, (UNIT, PLANE), 0) + experts[t] * UNIT
        spread.append(jnp.where(index.astype(F32) == place, 1.0, 0.0).astype(BF16))
    spread = jnp.concatenate(spread, axis=0)

    for k in (1, 3, 2):
        from_block = pl.ds(pl.multiple_of(((x + NX - k) % NX) * ROWS, ROWS), ROWS)
        remote(normed.at[:, own_rows], rows_in.at[from_block, :], nx_s.at[k - 1], nx_r.at[k - 1], at_x(k)).wait_recv()

    for c in range(4):
        cols = slice(c * 256, (c + 1) * 256)
        slotted = jnp.dot(spread, rows_in[:, cols], preferred_element_type=F32).astype(BF16)
        zsend[:, :, cols] = slotted.reshape(EXPS, UNIT, 256)
        w, j = PLACE[0]
        xin[w, j, :, cols] = slotted[:UNIT]

    def forward(t, src):
        w, j = PLACE[t]
        send(src, xin.at[w, 2 + j], f_s.at[t], f_r.at[t], partner)

    for t in SEND_ORDER:
        w, j = PLACE[t]
        send(zsend.at[t], xin.at[w, j], z_s.at[t], z_r.at[t], at_z(dest_offset(t)))
    forward(0, zsend.at[0])
    for k in (1, 3, 2):
        other_cols = pl.ds(pl.multiple_of(((x + k) % NX) * DX, DX), DX)
        send(wd.at[:, other_cols], wdn.at[own_hid, :], wx_s.at[2, k - 1], wx_r.at[2, k - 1], at_x(k))

    eye = early == late
    place_col = jnp.sum(jnp.where(eye, place, 0.0), axis=1, keepdims=True)
    column[...] = jnp.broadcast_to(
        jnp.sum(jnp.where(eye, plane_row(weights), 0.0), axis=1, keepdims=True), column.shape
    )
    key = lax.broadcasted_iota(jnp.int32, (PLANE, EXPS * UNIT), 1)
    shift = jnp.zeros_like(key)
    for t in range(EXPS):
        shift = jnp.where(key // UNIT == t, (experts[t] - t) * UNIT, shift)
    select[...] = jnp.where((key + shift).astype(F32) == place_col, 1.0, 0.0).astype(BF16)

    def wait_landed(wave):
        for t in WAVES[wave]:
            if t:
                w, j = PLACE[t]
                remote(zsend.at[t], xin.at[w, j], z_s.at[t], z_r.at[t], at_z(dest_offset(t))).wait_recv()
                forward(t, xin.at[w, j])

    def gate_up(wave):
        for t in WAVES[wave]:
            w, j = PLACE[t]
            remote(xin.at[w, j], xin.at[w, 2 + j], f_s.at[t], f_r.at[t], partner).wait_recv()
        if wave == 0:
            local[0].wait()
            local[1].wait()
            for k in (1, 3, 2):
                from_x = (x + NX - k) % NX
                cols_g = pl.ds(pl.multiple_of(from_x * 2 * HID, HID), HID)
                cols_u = pl.ds(pl.multiple_of(from_x * 2 * HID + HID, HID), HID)
                remote(wg.at[own_rows, :], wcat.at[:, cols_g], wx_s.at[0, k - 1], wx_r.at[0, k - 1], at_x(k)).wait_recv()
                remote(wu.at[own_rows, :], wcat.at[:, cols_u], wx_s.at[1, k - 1], wx_r.at[1, k - 1], at_x(k)).wait_recv()
        flat = xin[wave].reshape(4 * UNIT, DX)
        for c in range(4):
            cols = slice(c * 256, (c + 1) * 256)
            part = jnp.dot(flat, wcat[:, cols], preferred_element_type=F32).astype(BF16)
            rs_send[wave, :, :, cols] = part.reshape(4, UNIT, 256)
        for k in (1, 3, 2):
            send(rs_send.at[wave, (x + k) % NX], rs_recv.at[wave, k - 1], rs_s.at[wave, k - 1], rs_r.at[wave, k - 1], at_x(k))

    def activate(wave):
        for k in (1, 3, 2):
            remote(rs_send.at[wave, x], rs_recv.at[wave, k - 1], rs_s.at[wave, k - 1], rs_r.at[wave, k - 1], at_x(k)).wait_recv()
        for c in range(NX):
            cols = slice(c * 2 * HID, (c + 1) * 2 * HID)
            both = rs_send[wave, x, :, cols].astype(F32)
            for k in range(3):
                both = both + rs_recv[wave, k, :, cols].astype(F32)
            gate, up = both[:, :HID], both[:, HID:]
            hid[wave, x, :, c * HID:(c + 1) * HID] = (gate / (1.0 + jnp.exp(-gate)) * up).astype(BF16)
        for k in (1, 3, 2):
            send(hid.at[wave, x], hid.at[wave, x], hd_s.at[wave, k - 1], hd_r.at[wave, k - 1], at_x(k))

    def down(wave):
        for k in (1, 3, 2):
            remote(hid.at[wave, x], hid.at[wave, (x + NX - k) % NX], hd_s.at[wave, k - 1], hd_r.at[wave, k - 1], at_x(k)).wait_recv()
        if wave == 0:
            local[2].wait()
            for k in (1, 3, 2):
                from_hid = pl.ds(pl.multiple_of(((x + NX - k) % NX) * HID, HID), HID)
                remote(wd.at[:, own_rows], wdn.at[from_hid, :], wx_s.at[2, k - 1], wx_r.at[2, k - 1], at_x(k)).wait_recv()
        flat = hid[wave].reshape(4 * UNIT, NX * HID)
        for c in range(4):
            cols = slice(c * 256, (c + 1) * 256)
            part = jnp.dot(flat, wdn[:, cols], preferred_element_type=F32)
            for j, t in enumerate(WAVES[wave]):
                own_part[t, :, cols] = part[j * UNIT:(j + 1) * UNIT]
                pr_send[t, :, cols] = part[(2 + j) * UNIT:(3 + j) * UNIT].astype(BF16)
        for t in WAVES[wave]:
            send(pr_send.at[t], pr_recv.at[t], pr_s.at[t], pr_r.at[t], partner)

    def give_back(wave):
        for t in WAVES[wave]:
            remote(pr_send.at[t], pr_recv.at[t], pr_s.at[t], pr_r.at[t], partner).wait_recv()
            both = (own_part[t] + pr_recv[t].astype(F32)).astype(BF16)
            if t:
                ret_send[t] = both
                send(ret_send.at[t], ret_recv.at[t], rt_s.at[t], rt_r.at[t], at_z(source_offset(t)))
            else:
                ret_recv[t] = both

    wait_landed(0)
    gate_up(0)
    wait_landed(1)
    activate(0)
    gate_up(1)
    down(0)
    activate(1)
    give_back(0)
    wait_landed(2)
    down(1)
    gate_up(2)
    give_back(1)
    activate(2)
    wait_landed(3)
    down(2)
    gate_up(3)
    give_back(2)
    activate(3)
    down(3)
    give_back(3)

    for t in range(1, EXPS):
        remote(ret_send.at[t], ret_recv.at[t], rt_s.at[t], rt_r.at[t], at_z(source_offset(t))).wait_recv()
    for c in range(4):
        cols = slice(c * 256, (c + 1) * 256)
        back = ret_recv[:, :, cols].reshape(EXPS * UNIT, 256)
        rows = jnp.dot(select[...], back, preferred_element_type=F32)
        rows = rows * jnp.concatenate([column[...], column[...]], axis=1)
        eo_send[:, :, cols] = rows.astype(BF16).reshape(NX, ROWS, 256)
    for k in range(NX):
        xo = (x + k) % NX
        send(eo_send.at[xo], eo_recv.at[x], eo_s.at[k], eo_r.at[k], (sec_next, z * NX + xo))

    remote(tok, hprev, h_s, h_r, (sec_next, me)).wait_recv()
    for k in range(NX):
        xf = (x + NX - k) % NX
        remote(eo_send.at[x], eo_recv.at[xf], eo_s.at[k], eo_r.at[k], (sec_next, me)).wait_recv()
    for c in range(NX):
        cols = slice(c * DX, (c + 1) * DX)
        out[:, cols] = (hprev[:, cols].astype(F32) + eo_recv[c].astype(F32)).astype(BF16)
    for copy in pending:
        copy.wait_send()


def local(tokens, expert_ids, gate_weights, norm_gain, w_gate, w_up, w_down):
    vmem = pl.BlockSpec(memory_space=pltpu.VMEM)
    hbm = pl.BlockSpec(memory_space=pl.ANY)
    dma = pltpu.SemaphoreType.DMA
    scratch = [
        pltpu.VMEM((ROWS, D), BF16),
        pltpu.VMEM((PLANE, DX), BF16),
        pltpu.VMEM((EXPS, UNIT, DX), BF16),
        pltpu.VMEM((4, 4, UNIT, DX), BF16),
        pltpu.VMEM((DX, 2 * NX * HID), BF16),
        pltpu.VMEM((NX * HID, DX), BF16),
        pltpu.VMEM((4, NX, UNIT, 2 * NX * HID), BF16),
        pltpu.VMEM((4, 3, UNIT, 2 * NX * HID), BF16),
        pltpu.VMEM((4, NX, UNIT, NX * HID), BF16),
        pltpu.VMEM((EXPS, UNIT, DX), F32),
        pltpu.VMEM((EXPS, UNIT, DX), BF16),
        pltpu.VMEM((EXPS, UNIT, DX), BF16),
        pltpu.VMEM((EXPS, UNIT, DX), BF16),
        pltpu.VMEM((EXPS, UNIT, DX), BF16),
        pltpu.VMEM((NX, ROWS, DX), BF16),
        pltpu.VMEM((NX, ROWS, DX), BF16),
        pltpu.VMEM((ROWS, D), BF16),
        pltpu.VMEM((PLANE, EXPS * UNIT), BF16),
        pltpu.VMEM((PLANE, 128), F32),
        dma((3,)), dma((3,)), dma((3,)), dma((3, 3)), dma((3, 3)), dma(()), dma(()),
        dma((8,)), dma((8,)), dma((8,)), dma((8,)), dma((4, 3)), dma((4, 3)), dma((4, 3)), dma((4, 3)),
        dma((8,)), dma((8,)), dma((8,)), dma((8,)), dma((4,)), dma((4,)),
    ]
    result = pl.pallas_call(
        kernel,
        out_shape=jax.ShapeDtypeStruct((ROWS, D), BF16),
        in_specs=[vmem, vmem, vmem, vmem, hbm, hbm, hbm],
        out_specs=vmem,
        scratch_shapes=scratch,
        name="moe_stop",
        compiler_params=pltpu.CompilerParams(
            collective_id=0, has_side_effects=True, vmem_limit_bytes=48 * 1024 * 1024
        ),
    )(
        tokens[0],
        expert_ids.reshape(32, 128),
        gate_weights.reshape(32, 128),
        norm_gain,
        w_gate[0],
        w_up[0],
        w_down[0],
    )
    return result[None]


def solution(mesh):
    placed = (
        P("section", "expert", None),
        P("section", None, None, None),
        P("section", None, None, None),
        P("section", None),
        P("section", None, "expert"),
        P("section", None, "expert"),
        P("section", "expert", None),
    )
    return jax.shard_map(
        local, mesh=mesh, in_specs=placed, out_specs=P("section", "expert", None), check_vma=False
    )
```
